32 devices in a mesh: blocks: 2 (over y), rows: 4 (over z), cols: 4 (over x, core).
Axes of the slice: x: 2, y: 2, z: 4, core: 2. Of those that a mesh axis runs over, the one named last changes fastest.
Arguments:
- sens_tiles: bfloat16 [128, 1024, 256], P(('blocks', 'rows'), 'cols'), parts along dimension 0, may hold values from -10.606602 to 10.606602, as said below
- tile_coords: int32 [128, 8], P(('blocks', 'rows'), 'cols'), parts along dimension 0, may hold values from 0 to 7, as said below
- tile_counts: int32 [8, 4], P(('blocks', 'rows'), 'cols'), parts along dimension 0, may hold values from 3 to 16, as said below
- data_vec: float32 [192, 4096], P('blocks', 'rows'), parts along dimension 0, may hold values from -6 to 6
- cell_vec: float32 [192, 8192], P('blocks', 'cols'), parts along dimension 0, may hold values from -6 to 6
- alpha_now: float32 [192], P('blocks'), parts along dimension 0, may hold values from 0.5 to 2
Outputs:
- data_next: float32 [192, 4096], P('blocks', 'rows'), parts along dimension 0
- cell_next: float32 [192, 8192], P('blocks', 'cols'), parts along dimension 0
- beta_next: float32 [192], P('blocks'), parts along dimension 0
- alpha_next: float32 [192], P('blocks'), parts along dimension 0
The draws below stay inside these ranges and needn't reach their ends.
There are 2 independent parts, one for each index of `blocks`. The reference program is written for one: setup_inputs(seed, part) draws one part's arguments, and reference() takes and returns one part's arrays. A program takes and returns all parts, laid end to end along the dimension named above; each array names one. Nothing has to cross between parts.
Inputs may be any that keep to these rules, and one draw needn't show every extreme that they name: `sens_tiles`: entries of the tiles; slots at or beyond a device's count hold values that belong to no tile. `tile_coords`: within one device all 16 slots name distinct (row tile, column tile) pairs; the first entry of a pair is below 4, the second below 8. `tile_counts`: every data-row band has one device whose count is 16.
All inputs are finite; a program needn't handle non-finite values.
Results may differ from the reference program's by a relative error of at most 0.0043.
Values sent between devices are 32-bit elements; how exact they have to be, the bound alone decides.
No kernel may reach another device: no remote copies, remote signals or barrier semaphores. Data moves between devices by JAX's collectives and lax.ppermute only.
A program may use at most 64 MiB of HBM per device.

```python
import math
import jax
import jax.numpy as jnp
from jax import lax

TILE = 256
RT = 4
CT = 8
TMAX = 16
SAMPLES = 96
ROW_BANDS = 4
COL_BANDS = 4
DATA = 4096
CELLS = 8192


def draw_sens_tiles(key, part):
    rows_total = ROW_BANDS * TMAX
    key_noise, key_rows, key_cols = jax.random.split(key, 3)
    shape_four = (rows_total, COL_BANDS, TILE, TILE)
    noise = jnp.clip(jax.random.normal(key_noise, shape_four, jnp.float32), -6.0, 6.0)
    lowest, highest = (0.3, 3.0)
    row_scale = jnp.exp(jax.random.uniform(key_rows, (rows_total, COL_BANDS, TILE, 1), jnp.float32, math.log(lowest), math.log(highest)))
    col_scale = jnp.exp(jax.random.uniform(key_cols, (rows_total, COL_BANDS, 1, TILE), jnp.float32, math.log(lowest), math.log(highest)))
    row_band = (jnp.arange(rows_total) // TMAX).astype(jnp.float32) / max(ROW_BANDS - 1, 1)
    col_band = jnp.arange(COL_BANDS).astype(jnp.float32) / max(COL_BANDS - 1, 1)
    band_factor = 3.0 ** (0.5 * (row_band[:, None] + col_band[None, :]))
    values = noise * row_scale * col_scale * band_factor[:, :, None, None] / math.sqrt(TILE * CT)
    return values.reshape(rows_total, COL_BANDS * TILE, TILE).astype(jnp.bfloat16)


def draw_tile_coords(key, part):
    device_keys = jax.random.split(key, ROW_BANDS * COL_BANDS)
    orders = jax.vmap(lambda one_key: jax.random.permutation(one_key, RT * CT))(device_keys)[:, :TMAX]
    stacked = jnp.stack([orders // CT, orders % CT], axis=-1)
    stacked = stacked.reshape(ROW_BANDS, COL_BANDS, TMAX, 2).transpose(0, 2, 1, 3)
    return stacked.reshape(ROW_BANDS * TMAX, COL_BANDS * 2).astype(jnp.int32)


def draw_tile_counts(key, part):
    key_base, key_full = jax.random.split(key, 2)
    base = jax.random.randint(key_base, (ROW_BANDS, COL_BANDS), TMAX // 8 + 1, TMAX * 5 // 8 + 1, jnp.int32)
    chosen = jax.random.randint(key_full, (ROW_BANDS, 1), 0, COL_BANDS, jnp.int32)
    columns = jnp.arange(COL_BANDS, dtype=jnp.int32)[None, :]
    return jnp.where(columns == chosen, TMAX, base).astype(jnp.int32)


def block_levels(key, shape, cuts, smallest, top_value):
    def one(position, parts):
        steps = jax.random.uniform(jax.random.fold_in(jax.random.fold_in(key, 6), position), (parts,), jnp.float32, smallest / len(cuts), top_value / len(cuts))
        return jnp.repeat(jnp.exp(steps), shape[position] // parts).reshape((-1,) + (1,) * (len(shape) - position - 1))

    factor_of = one(*cuts[0])
    for cut in cuts[1:]:
        factor_of = factor_of * one(*cut)
    return factor_of


def bell_draw(stream_key, extent, scale, bound, cuts=(), held_as=jnp.bfloat16):
    level = block_levels(stream_key, extent, cuts, -0.22, 0.18) if cuts else 1.0
    entries = jax.random.normal(stream_key, extent, jnp.float32) * scale * level
    return jnp.minimum(jnp.maximum(entries, -bound), bound).astype(held_as)


def setup_inputs(seed: int = 0, part: int = 0) -> dict:
    arg_keys = jax.random.split(jax.random.key(seed), 7)
    part_splits = jax.random.split(jax.random.fold_in(arg_keys[6], part), 7)
    sens_tiles = draw_sens_tiles(jax.random.fold_in(jax.random.fold_in(arg_keys[6], part), 71), part)
    tile_coords = draw_tile_coords(jax.random.fold_in(jax.random.fold_in(arg_keys[6], part), 71), part)
    tile_counts = draw_tile_counts(jax.random.fold_in(jax.random.fold_in(arg_keys[6], part), 71), part)
    data_vec = bell_draw(part_splits[3], (SAMPLES, DATA), 1.0, 6.0, ((1, 4),), jnp.float32)
    cell_vec = bell_draw(part_splits[4], (SAMPLES, CELLS), 1.0, 6.0, ((1, 4),), jnp.float32)
    alpha_now = jnp.clip(jnp.exp(jax.random.uniform(part_splits[5], (SAMPLES,), jnp.float32, math.log(0.5), math.log(2.0))), 0.5, 2.0)
    return {"sens_tiles": sens_tiles, "tile_coords": tile_coords, "tile_counts": tile_counts, "data_vec": data_vec, "cell_vec": cell_vec, "alpha_now": alpha_now}


EPSILON = 1e-06

def arrange(sens_tiles, tile_coords, tile_counts):
    layered = sens_tiles.reshape(ROW_BANDS, TMAX, COL_BANDS, TILE, TILE).transpose(0, 2, 1, 3, 4)
    places = tile_coords.reshape(ROW_BANDS, TMAX, COL_BANDS, 2).transpose(0, 2, 1, 3)
    listed = (jnp.arange(TMAX, dtype=jnp.int32)[None, None, :] < tile_counts[:, :, None]).astype(jnp.float32)
    return (layered, places, listed)

def forward_product(layered, places, listed, cell_low):
    cell_blocks = cell_low.astype(jnp.float32).reshape(SAMPLES, COL_BANDS, CT, TILE)

    def one_band(operands):
        band_tiles, band_places, band_listed = operands
        picked = jnp.take_along_axis(cell_blocks, band_places[None, :, :, 1, None].astype(jnp.int32), axis=2)
        contrib = jnp.einsum('kctj,ctij->kcti', picked, band_tiles.astype(jnp.float32), precision=lax.Precision.HIGHEST)
        spread = jax.nn.one_hot(band_places[:, :, 0], RT, dtype=jnp.float32) * band_listed[:, :, None]
        return jnp.einsum('kcti,ctr->kri', contrib, spread, precision=lax.Precision.HIGHEST)
    banded = lax.map(one_band, (layered, places, listed))
    return banded.transpose(1, 0, 2, 3).reshape(SAMPLES, ROW_BANDS * RT * TILE)

def adjoint_product(layered, places, listed, data_low):
    row_blocks = data_low.astype(jnp.float32).reshape(SAMPLES, ROW_BANDS, RT, TILE).transpose(1, 0, 2, 3)

    def one_band(running, operands):
        band_rows, band_tiles, band_places, band_listed = operands
        picked = jnp.take(band_rows, band_places[:, :, 0].astype(jnp.int32), axis=1)
        contrib = jnp.einsum('kcti,ctij->kctj', picked, band_tiles.astype(jnp.float32), precision=lax.Precision.HIGHEST)
        spread = jax.nn.one_hot(band_places[:, :, 1], CT, dtype=jnp.float32) * band_listed[:, :, None]
        return (running + jnp.einsum('kctj,cts->kcsj', contrib, spread, precision=lax.Precision.HIGHEST), None)
    empty_sum = jnp.zeros((SAMPLES, COL_BANDS, CT, TILE), jnp.float32)
    running, _ = lax.scan(one_band, empty_sum, (row_blocks, layered, places, listed))
    return running.reshape(SAMPLES, COL_BANDS * CT * TILE)

def reference(sens_tiles, tile_coords, tile_counts, data_vec, cell_vec, alpha_now):
    layered, places, listed = arrange(sens_tiles, tile_coords, tile_counts)
    forward = forward_product(layered, places, listed, cell_vec.astype(jnp.bfloat16))
    residual = forward - alpha_now[:, None] * data_vec
    beta_next = jnp.sqrt(lax.optimization_barrier(jnp.sum(residual * residual, axis=1)) / DATA + EPSILON)
    data_next = residual / beta_next[:, None]
    backward = adjoint_product(layered, places, listed, data_next.astype(jnp.bfloat16))
    fresh = backward - beta_next[:, None] * cell_vec
    alpha_next = jnp.sqrt(lax.optimization_barrier(jnp.sum(fresh * fresh, axis=1)) / CELLS + EPSILON)
    cell_next = fresh / alpha_next[:, None]
    return (data_next, cell_next, beta_next, alpha_next)
```

```python
import functools

import jax
import jax.numpy as jnp
from jax import lax
from jax.experimental import pallas as pl
from jax.experimental.pallas import tpu as pltpu
from jax.sharding import PartitionSpec as P

EPSILON = 1e-06
LANES = 128
CHUNKS = 4
GRANT = pltpu.CompilerParams(vmem_limit_bytes=12 << 20)

F32 = jnp.float32
BF16 = jnp.bfloat16
NT = (((1,), (1,)), ((), ()))
NN = (((1,), (0,)), ((), ()))


def vmem():
    return pl.BlockSpec(memory_space=pltpu.VMEM)


def smem():
    return pl.BlockSpec(memory_space=pltpu.SMEM)


def diagonal(samples):
    rows = lax.broadcasted_iota(jnp.int32, (samples, LANES), 0)
    lanes = lax.broadcasted_iota(jnp.int32, (samples, LANES), 1)
    return rows == lanes


def as_row(column):
    picked = jnp.where(diagonal(column.shape[0]), column, 0.0)
    return jnp.sum(picked, axis=0, keepdims=True)


def as_column(row, samples):
    picked = jnp.where(diagonal(samples), row, 0.0)
    return jnp.sum(picked, axis=1, keepdims=True)


def forward_kernel(coords, count, cell_ref, tiles_ref, *rest):
    outs, cells, acc = rest[:-2], rest[-2], rest[-1]
    slots, tile = tiles_ref.shape[:2]
    part_samples = outs[0].shape[0]
    for c in range(cells.shape[0]):
        cells[c] = cell_ref[:, c * tile : (c + 1) * tile].astype(BF16)
    acc[...] = jnp.zeros_like(acc)
    for t in range(slots):
        part = lax.dot_general(cells[coords[t, 1]], tiles_ref[t], NT, preferred_element_type=F32)
        acc[coords[t, 0]] += jnp.where(t < count[0, 0], part, 0.0)
    for m, out in enumerate(outs):
        for r in range(acc.shape[0]):
            out[:, r * tile : (r + 1) * tile] = acc[r, m * part_samples : (m + 1) * part_samples]


def forward(coords, count, cell_vec, tiles, row_tiles, chunks):
    samples, cells = cell_vec.shape
    tile = tiles.shape[1]
    return pl.pallas_call(
        forward_kernel,
        out_shape=[jax.ShapeDtypeStruct((samples // chunks, row_tiles * tile), F32)] * chunks,
        in_specs=[smem(), smem(), vmem(), vmem()],
        out_specs=[vmem()] * chunks,
        scratch_shapes=[
            pltpu.VMEM((cells // tile, samples, tile), BF16),
            pltpu.VMEM((row_tiles, samples, tile), F32),
        ],
        compiler_params=GRANT,
        name="forward",
    )(coords, count, cell_vec, tiles)


def backward_kernel(m, coords, count, half, ours, theirs, data_ref, alpha_ref, tiles_ref, keep, send, residual, squares, low, acc):
    slots, tile = tiles_ref.shape[:2]
    samples = ours.shape[0]
    rows = slice(m * samples, (m + 1) * samples)
    value = ours[...] + theirs[...] - alpha_ref[rows] * data_ref[rows]
    residual[...] = value
    squares[...] = as_row(jnp.sum(value * value, axis=1, keepdims=True))
    for r in range(low.shape[0]):
        low[r] = value[:, r * tile : (r + 1) * tile].astype(BF16)
    acc[...] = jnp.zeros_like(acc)
    for t in range(slots):
        part = lax.dot_general(low[coords[t, 0]], tiles_ref[t], NN, preferred_element_type=F32)
        acc[coords[t, 1]] += jnp.where(t < count[0, 0], part, 0.0)
    width = acc.shape[0] // 2
    for c in range(width):
        keep[:, c * tile : (c + 1) * tile] = acc[half[0] * width + c]
        send[:, c * tile : (c + 1) * tile] = acc[(1 - half[0]) * width + c]


def backward(m, coords, count, half, ours, theirs, data_vec, alpha, tiles, col_tiles):
    samples, data = ours.shape
    tile = tiles.shape[1]
    piece = jax.ShapeDtypeStruct((samples, col_tiles * tile // 2), F32)
    return pl.pallas_call(
        functools.partial(backward_kernel, m),
        out_shape=[
            piece,
            piece,
            jax.ShapeDtypeStruct((samples, data), F32),
            jax.ShapeDtypeStruct((1, LANES), F32),
        ],
        in_specs=[smem()] * 3 + [vmem()] * 5,
        out_specs=[vmem()] * 4,
        scratch_shapes=[
            pltpu.VMEM((data // tile, samples, tile), BF16),
            pltpu.VMEM((col_tiles, samples, tile), F32),
        ],
        compiler_params=GRANT,
        name=f"backward_{m}",
    )(coords, count, half, ours, theirs, data_vec, alpha, tiles)


def fresh_kernel(m, total, half, ours, theirs, sums, cell_ref, fresh, squares):
    samples, width = ours.shape
    beta = jnp.sqrt(as_column(sums[m : m + 1], samples) / total + EPSILON)
    cells = cell_ref[m * samples : (m + 1) * samples, pl.ds(pl.multiple_of(half[0] * width, LANES), width)]
    value = (ours[...] + theirs[...]) / beta - beta * cells
    fresh[...] = value
    squares[...] = as_row(jnp.sum(value * value, axis=1, keepdims=True))


def fresh_piece(m, total, half, ours, theirs, sums, cell_vec):
    return pl.pallas_call(
        functools.partial(fresh_kernel, m, total),
        out_shape=[jax.ShapeDtypeStruct(ours.shape, F32), jax.ShapeDtypeStruct((1, LANES), F32)],
        in_specs=[smem()] + [vmem()] * 4,
        out_specs=[vmem()] * 2,
        compiler_params=GRANT,
        name=f"fresh_{m}",
    )(half, ours, theirs, sums, cell_vec)


def data_kernel(total, sums, *rest):
    chunks = sums.shape[0]
    residuals, out, beta_row = rest[:chunks], rest[chunks], rest[chunks + 1]
    samples = residuals[0].shape[0]
    beta_row[...] = jnp.sqrt(sums[...] / total + EPSILON)
    for m in range(chunks):
        beta = jnp.sqrt(as_column(sums[m : m + 1], samples) / total + EPSILON)
        out[m * samples : (m + 1) * samples] = residuals[m][...] / beta


def data_out(total, sums, residuals):
    samples, data = residuals[0].shape
    return pl.pallas_call(
        functools.partial(data_kernel, total),
        out_shape=[
            jax.ShapeDtypeStruct((samples * len(residuals), data), F32),
            jax.ShapeDtypeStruct(sums.shape, F32),
        ],
        in_specs=[vmem()] * (1 + len(residuals)),
        out_specs=[vmem()] * 2,
        compiler_params=GRANT,
        name="data_out",
    )(sums, *residuals)


def cell_kernel(total, half, sums, *rest):
    chunks = sums.shape[0]
    ours, theirs = rest[:chunks], rest[chunks : 2 * chunks]
    out, alpha_row = rest[2 * chunks :]
    samples, width = ours[0].shape
    alpha_row[...] = jnp.sqrt(sums[...] / total + EPSILON)
    for m in range(chunks):
        rows = slice(m * samples, (m + 1) * samples)
        scale = 1.0 / jnp.sqrt(as_column(sums[m : m + 1], samples) / total + EPSILON)
        out[rows, pl.ds(pl.multiple_of(half[0] * width, LANES), width)] = ours[m][...] * scale
        out[rows, pl.ds(pl.multiple_of((1 - half[0]) * width, LANES), width)] = theirs[m][...] * scale


def cell_out(total, half, sums, ours, theirs):
    samples, width = ours[0].shape
    return pl.pallas_call(
        functools.partial(cell_kernel, total),
        out_shape=[
            jax.ShapeDtypeStruct((samples * len(ours), 2 * width), F32),
            jax.ShapeDtypeStruct(sums.shape, F32),
        ],
        in_specs=[smem(), vmem()] + [vmem()] * (2 * len(ours)),
        out_specs=[vmem()] * 2,
        compiler_params=GRANT,
        name="cell_out",
    )(half, sums, *ours, *theirs)


def bits_of(axis):
    size = lax.axis_size(axis)
    if size < 2 or size & (size - 1):
        raise ValueError("axis size")
    return [1 << b for b in range(size.bit_length() - 1)]


def swap(value, axis, bit):
    return lax.ppermute(value, axis, [(i, i ^ bit) for i in range(lax.axis_size(axis))])


def add_up(value, axis, bits):
    for bit in bits:
        value = value + swap(value, axis, bit)
    return value


def spread_rows(rows, samples):
    return rows[:, :samples].reshape(-1)


def per_device(sens_tiles, tile_coords, tile_counts, data_vec, cell_vec, alpha_now):
    tile = sens_tiles.shape[1]
    samples = data_vec.shape[0]
    row_tiles = data_vec.shape[1] // tile
    col_tiles = cell_vec.shape[1] // tile
    chunks = CHUNKS
    part = samples // chunks
    data_total = data_vec.shape[1] * lax.axis_size("rows")
    cell_total = cell_vec.shape[1] * lax.axis_size("cols")
    row_bits, col_bits = bits_of("rows"), bits_of("cols")
    half = (lax.axis_index("rows") % 2).astype(jnp.int32).reshape(1)
    alpha = alpha_now[:, None]

    partial = forward(tile_coords, tile_counts, cell_vec, sens_tiles, row_tiles, chunks)
    ours = [add_up(p, "cols", col_bits[:0:-1]) for p in partial]
    theirs = [swap(p, "cols", col_bits[0]) for p in ours]
    keeps, sends, residuals, squares = zip(
        *[
            backward(m, tile_coords, tile_counts, half, ours[m], theirs[m], data_vec, alpha, sens_tiles, col_tiles)
            for m in range(chunks)
        ]
    )
    pieces = [keep + swap(send, "rows", row_bits[0]) for keep, send in zip(keeps, sends)]
    data_sums = add_up(jnp.concatenate(squares, 0), "rows", row_bits)
    pieces = [add_up(p, "rows", row_bits[1:-1]) for p in pieces]
    others = [swap(p, "rows", row_bits[-1]) for p in pieces]
    data_next, beta_rows = data_out(data_total, data_sums, residuals)
    fresh, cell_squares = zip(
        *[fresh_piece(m, data_total, half, pieces[m], others[m], data_sums, cell_vec) for m in range(chunks)]
    )
    cell_sums = add_up(jnp.concatenate(cell_squares, 0), "cols", col_bits)
    cell_sums = add_up(cell_sums, "rows", row_bits[:1])
    gathered = [swap(f, "rows", row_bits[0]) for f in fresh]
    cell_next, alpha_rows = cell_out(cell_total, half, cell_sums, fresh, gathered)
    return (data_next, cell_next, spread_rows(beta_rows, part), spread_rows(alpha_rows, part))


def solution(mesh):
    placed = (
        P(("blocks", "rows"), "cols", None),
        P(("blocks", "rows"), "cols"),
        P(("blocks", "rows"), "cols"),
        P("blocks", "rows"),
        P("blocks", "cols"),
        P("blocks"),
    )
    return jax.shard_map(
        per_device,
        mesh=mesh,
        in_specs=placed,
        out_specs=(P("blocks", "rows"), P("blocks", "cols"), P("blocks"), P("blocks")),
        check_vma=False,
    )
```
